32 devices in a mesh: dp: 4 (over z), tensor: 8 (over y, x, core).
Axes of the slice: x: 2, y: 2, z: 4, core: 2. Of those that a mesh axis runs over, the one named last changes fastest.
Arguments:
- tokens_in: bfloat16 [4096, 1024], P(('dp', 'tensor')), may hold values from -6 to 6
- ln_gain: float32 [2, 2, 1024], replicated, may hold values from 0.5 to 1.5
- ln_bias: float32 [2, 2, 1024], replicated, may hold values from -2 to 2
- w_qkv: bfloat16 [2, 1024, 3072], P(None, None, 'tensor')
- b_qv: float32 [2, 2048], P(None, 'tensor'), may hold values from -3 to 3
- w_out: bfloat16 [2, 1024, 1024], P(None, 'tensor'), may hold values from -1.5 to 1.5
- b_resid: float32 [2, 1024], replicated, may hold values from -2 to 2
- w_up: bfloat16 [2, 1024, 4096], P(None, None, 'tensor'), may hold values from -0.1875 to 0.1875
- b_up: float32 [2, 4096], P(None, 'tensor'), may hold values from -3 to 3
- w_down: bfloat16 [2, 4096, 1024], P(None, 'tensor'), may hold values from -0.09375 to 0.09375
- segments: int32 [4, 1024], P('dp'), may hold values from 0 to 3, never falling along the last dimension, each value on 1 to 512 neighbouring positions
- cotangent: bfloat16 [4096, 1024], P(('dp', 'tensor')), may hold values from -6 to 6
Outputs:
- result: bfloat16 [4096, 1024], P(('dp', 'tensor'))
- grad_tokens: float32 [4096, 1024], P(('dp', 'tensor'))
- grad_ln_gain: float32 [2, 2, 1024], replicated
- grad_ln_bias: float32 [2, 2, 1024], replicated
- grad_w_qkv: float32 [2, 1024, 3072], P(None, None, 'tensor')
- grad_b_qv: float32 [2, 2048], P(None, 'tensor')
- grad_w_out: float32 [2, 1024, 1024], P(None, 'tensor')
- grad_b_resid: float32 [2, 1024], replicated
- grad_w_up: float32 [2, 1024, 4096], P(None, None, 'tensor')
- grad_b_up: float32 [2, 4096], P(None, 'tensor')
- grad_w_down: float32 [2, 4096, 1024], P(None, 'tensor')
The draws below stay inside these ranges and needn't reach their ends.
Inputs may be any that keep to these rules, and one draw needn't show every extreme that they name: `segments`: in each packed sequence the document numbers start at 0 and never fall; every document has 1 to 512 tokens.
All inputs are finite; a program needn't handle non-finite values.
Results may differ from the reference program's by a relative error of at most 0.014.
Values may be sent and summed in bfloat16 or wider, within the bound.
No kernel may reach another device: no remote copies, remote signals or barrier semaphores. Data moves between devices by JAX's collectives and lax.ppermute only.
A program may use at most 128 MiB of HBM per device.

```python
import math
import jax
import jax.numpy as jnp
import numpy as np
from jax import lax

D = 1024
HEADS = 16
HD = 64
ROT = 16
FF = 4096
LAYERS = 2
L = 1024
SEQS = 4
TOKENS = 4096


def draw_w_qkv(key, part):
    base = jax.random.normal(key, (LAYERS, D, HEADS, 3, HD), jnp.float32) * D ** (-0.5)
    return base.reshape(LAYERS, D, HEADS * 3 * HD).astype(jnp.bfloat16)


def levels(own_key, dims, shards, least, top_value):
    factor_of, own = 1.0, jax.random.fold_in(own_key, 6)
    for axis_at, parts in shards:
        steps = jnp.exp(jax.random.uniform(jax.random.fold_in(own, axis_at), (parts,), jnp.float32, least / len(shards), top_value / len(shards)))
        factor_of = factor_of * jnp.repeat(steps, dims[axis_at] // parts).reshape([-1 if axis == axis_at else 1 for axis in range(len(dims))])
    return factor_of


def split_up(amount, total, limit, skew):
    loads = [(1 << 20) // math.isqrt(grade ** skew) + 1 for grade in range(2, amount + 1)]
    spare, counts = total - limit - (amount - 1), [1] * (amount - 1)
    while spare > 0:
        movable = [i for i in range(amount - 1) if counts[i] < limit]
        mass, left = sum([loads[i] for i in movable]), spare
        for i in movable:
            more = min(limit - counts[i], max(1, left * loads[i] // mass), spare)
            counts[i] = counts[i] + more
            spare = spare - more
    return np.array([limit] + counts)


def uneven_parts(stream_key, amount, total, limit, lean):
    if amount == 2:
        one = jax.random.randint(stream_key, (), max(1, total - limit), min(limit, total - 1) + 1)
        return jnp.stack([one, total - one])
    sizes = jnp.asarray(split_up(amount, total, limit, lean), jnp.int32)
    twos = (amount - 1) // 2
    source_of, taker = sizes[1:1 + 2 * twos:2], sizes[2:2 + 2 * twos:2]
    margin = jnp.minimum(source_of - 1, limit - taker)
    passed = jax.random.randint(jax.random.fold_in(stream_key, 1), (twos,), 0, 1 << 20) % (margin + 1)
    sizes = sizes.at[1:1 + 2 * twos:2].set(source_of - passed).at[2:2 + 2 * twos:2].set(taker + passed)
    return sizes[jax.random.permutation(jax.random.fold_in(stream_key, 2), amount)]


def noise(stream_key, extent, width, most, split=(), kind=jnp.bfloat16):
    array = jax.random.normal(stream_key, extent, jnp.float32) * width
    if len(split) > 0:
        array = levels(stream_key, extent, split, -0.22, 0.18) * array
    return jnp.clip(array, min=-most, max=most).astype(kind)


def setup_inputs(seed: int = 0) -> dict:
    key_list = jax.random.split(jax.random.key(seed), 13)
    return {
        "tokens_in": noise(key_list[0], (TOKENS, D), 1.0, 6.0, ((0, 32),)),
        "ln_gain": jnp.clip(1.0 + 0.1 * jax.random.normal(key_list[1], (LAYERS, 2, D), jnp.float32), 0.5, 1.5),
        "ln_bias": noise(key_list[2], (LAYERS, 2, D), 0.3, 2.0, (), jnp.float32),
        "w_qkv": draw_w_qkv(jax.random.fold_in(key_list[12], 71), 0),
        "b_qv": noise(key_list[4], (LAYERS, HEADS * 2 * HD), 0.5, 3.0, ((1, 8),), jnp.float32),
        "w_out": noise(key_list[5], (LAYERS, HEADS * HD, D), (D // 64) ** -0.5, 1.5, ((1, 8),)),
        "b_resid": noise(key_list[6], (LAYERS, D), 0.3, 2.0, (), jnp.float32),
        "w_up": noise(key_list[7], (LAYERS, D, FF), D ** -0.5, 0.1875, ((2, 8),)),
        "b_up": noise(key_list[8], (LAYERS, FF), 0.5, 3.0, ((1, 8),), jnp.float32),
        "w_down": noise(key_list[9], (LAYERS, FF, D), FF ** -0.5, 0.09375, ((1, 8),)),
        "segments": jax.vmap(lambda own: jnp.searchsorted(jnp.cumsum(uneven_parts(own, 4, L, L // 2, 0)), jnp.arange(L), side="right"))(jax.random.split(key_list[10], SEQS)).reshape((SEQS, L)).astype(jnp.int32),
        "cotangent": noise(key_list[11], (TOKENS, D), 1.0, 6.0, ((0, 32),)),
    }


EPS = 1e-05

def norm_forward(rows, gain, shift):
    mean = lax.optimization_barrier(jnp.mean(rows, axis=-1, keepdims=True))
    centred = rows - mean
    var = lax.optimization_barrier(jnp.mean(centred * centred, axis=-1, keepdims=True))
    scale = lax.rsqrt(var + EPS)
    normal = centred * scale
    return (normal * gain + shift, normal, scale)

def norm_backward(upstream, normal, scale, gain):
    weighted = upstream * gain
    inner = weighted - lax.optimization_barrier(jnp.mean(weighted, axis=-1, keepdims=True)) - normal * lax.optimization_barrier(jnp.mean(weighted * normal, axis=-1, keepdims=True))
    return (inner * scale, lax.optimization_barrier(jnp.sum(upstream * normal, axis=0)), lax.optimization_barrier(jnp.sum(upstream, axis=0)))

def positions(segments):
    length = segments.shape[-1]
    index = jnp.broadcast_to(jnp.arange(length, dtype=jnp.int32), segments.shape)
    starts = jnp.concatenate([jnp.ones_like(segments[:, :1]), (segments[:, 1:] != segments[:, :-1]).astype(jnp.int32)], axis=1)
    first = lax.cummax(jnp.where(starts > 0, index, 0), axis=1)
    return (index - first).astype(jnp.int32)

def rotary_tables(pos, half):
    freq = 10000.0 ** (-jnp.arange(half, dtype=jnp.float32) / half)
    angle = pos.astype(jnp.float32)[..., None] * freq
    return (jnp.cos(angle)[:, :, None, :], jnp.sin(angle)[:, :, None, :])

def rotate(values, cos_t, sin_t, half, sign):
    first = values[..., :half]
    second = values[..., half:2 * half]
    new_first = first * cos_t - sign * second * sin_t
    new_second = second * cos_t + sign * first * sin_t
    return jnp.concatenate([new_first, new_second, values[..., 2 * half:]], axis=-1)

def gelu_slope(pre_act):
    cdf = 0.5 * (1.0 + lax.erf(pre_act * 0.7071067811865476))
    density = jnp.exp(-0.5 * pre_act * pre_act) * 0.3989422804014327
    return cdf + pre_act * density

def fdot(form, left, right):
    return jnp.einsum(form, left.astype(jnp.float32), right.astype(jnp.float32), precision=lax.Precision.HIGHEST)

def allowed_mask(start, block, seg_query, seg_all):
    length = seg_all.shape[0]
    rows = start + jnp.arange(block, dtype=jnp.int32)
    cols = jnp.arange(length, dtype=jnp.int32)
    return (cols[None, :] <= rows[:, None]) & (seg_query[:, None] == seg_all[None, :])

def attend_forward(query, keys, values, seg):
    length, heads, size = query.shape
    block = min(512, length)
    scale = size ** (-0.5)
    starts = jnp.arange(length // block, dtype=jnp.int32) * block

    def one(start):
        q_blk = lax.dynamic_slice_in_dim(query, start, block, 0)
        s_blk = lax.dynamic_slice_in_dim(seg, start, block, 0)
        scores = fdot('qhd,khd->hqk', q_blk, keys) * scale
        scores = jnp.where(allowed_mask(start, block, s_blk, seg)[None], scores, -1e+30)
        top = lax.optimization_barrier(jnp.max(scores, axis=-1, keepdims=True))
        expd = jnp.exp(scores - top)
        total = lax.optimization_barrier(jnp.sum(expd, axis=-1, keepdims=True))
        probs = (expd / total).astype(jnp.bfloat16)
        mixed = fdot('hqk,khd->qhd', probs, values)
        return (mixed.astype(jnp.bfloat16), (top + jnp.log(total))[..., 0])
    mixed, lse = lax.map(one, starts)
    return (mixed.reshape(length, heads, size), lse)

def attend_backward(query, keys, values, mixed, d_mixed, lse, seg):
    length, heads, size = query.shape
    block = min(512, length)
    scale = size ** (-0.5)
    starts = jnp.arange(length // block, dtype=jnp.int32) * block

    def step(carry, inputs):
        d_keys, d_values = carry
        start, lse_blk = inputs
        q_blk = lax.dynamic_slice_in_dim(query, start, block, 0)
        o_blk = lax.dynamic_slice_in_dim(mixed, start, block, 0)
        g_blk = lax.dynamic_slice_in_dim(d_mixed, start, block, 0)
        s_blk = lax.dynamic_slice_in_dim(seg, start, block, 0)
        scores = fdot('qhd,khd->hqk', q_blk, keys) * scale
        scores = jnp.where(allowed_mask(start, block, s_blk, seg)[None], scores, -1e+30)
        probs = jnp.exp(scores - lse_blk[:, :, None])
        delta = lax.optimization_barrier(jnp.sum(o_blk.astype(jnp.float32) * g_blk.astype(jnp.float32), axis=-1)).T
        d_values = d_values + fdot('hqk,qhd->khd', probs.astype(jnp.bfloat16), g_blk)
        d_probs = fdot('qhd,khd->hqk', g_blk, values)
        d_scores = (probs * (d_probs - delta[:, :, None]) * scale).astype(jnp.bfloat16)
        d_query = fdot('hqk,khd->qhd', d_scores, keys)
        d_keys = d_keys + fdot('hqk,qhd->khd', d_scores, q_blk)
        return ((d_keys, d_values), d_query)
    zeros = jnp.zeros((length, heads, size), jnp.float32)
    (d_keys, d_values), d_query = lax.scan(step, (zeros, zeros), (starts, lse))
    return (d_query.reshape(length, heads, size), d_keys, d_values)

def project(attn_in, w_qkv, b_qv, cos_t, sin_t, seqs, length):
    heads = w_qkv.shape[1] // (3 * HD)
    proj = jnp.dot(attn_in, w_qkv, preferred_element_type=jnp.float32).reshape(seqs, length, heads, 3, HD)
    bias = b_qv.reshape(heads, 2, HD)
    half = ROT // 2
    query = rotate(proj[:, :, :, 0] + bias[:, 0], cos_t, sin_t, half, 1.0)
    keys = rotate(proj[:, :, :, 1], cos_t, sin_t, half, 1.0)
    values = proj[:, :, :, 2] + bias[:, 1]
    return (query.astype(jnp.bfloat16), keys.astype(jnp.bfloat16), values.astype(jnp.bfloat16))

def layer_forward(hidden, params, cos_t, sin_t, segments):
    gain, shift, w_qkv, b_qv, w_out, b_resid, w_up, b_up, w_down = params
    seqs, length = segments.shape
    attn_f, attn_normal, attn_scale = norm_forward(hidden, gain[0], shift[0])
    mlp_f, mlp_normal, mlp_scale = norm_forward(hidden, gain[1], shift[1])
    attn_in = attn_f.astype(jnp.bfloat16)
    mlp_in = mlp_f.astype(jnp.bfloat16)
    query, keys, values = project(attn_in, w_qkv, b_qv, cos_t, sin_t, seqs, length)
    mixed, lse = lax.map(lambda xs: attend_forward(*xs), (query, keys, values, segments))
    mixed_flat = mixed.reshape(seqs * length, -1)
    branch = jnp.dot(mixed_flat, w_out, preferred_element_type=jnp.float32)
    pre_act = jnp.dot(mlp_in, w_up, preferred_element_type=jnp.float32) + b_up
    act = jax.nn.gelu(pre_act, approximate=False).astype(jnp.bfloat16)
    branch = branch + jnp.dot(act, w_down, preferred_element_type=jnp.float32)
    record = {'attn_in': attn_in, 'mlp_in': mlp_in, 'attn_normal': attn_normal, 'attn_scale': attn_scale, 'mlp_normal': mlp_normal, 'mlp_scale': mlp_scale, 'query': query, 'keys': keys, 'values': values, 'mixed': mixed, 'lse': lse}
    return (hidden + branch + b_resid, record)

def layer_backward(d_hidden, params, record, cos_t, sin_t, segments):
    gain, shift, w_qkv, b_qv, w_out, b_resid, w_up, b_up, w_down = params
    seqs, length = segments.shape
    d_resid_bias = lax.optimization_barrier(jnp.sum(d_hidden, axis=0))
    d_branch = d_hidden.astype(jnp.bfloat16)
    attn_in, mlp_in = (record['attn_in'], record['mlp_in'])
    pre_act = jnp.dot(mlp_in, w_up, preferred_element_type=jnp.float32) + b_up
    act = jax.nn.gelu(pre_act, approximate=False).astype(jnp.bfloat16)
    d_act = jnp.dot(d_branch, w_down.T, preferred_element_type=jnp.float32)
    d_w_down = jnp.dot(act.T, d_branch, preferred_element_type=jnp.float32)
    d_pre = d_act * gelu_slope(pre_act)
    d_pre_b = d_pre.astype(jnp.bfloat16)
    d_w_up = jnp.dot(mlp_in.T, d_pre_b, preferred_element_type=jnp.float32)
    d_b_up = lax.optimization_barrier(jnp.sum(d_pre, axis=0))
    d_mlp_in = jnp.dot(d_pre_b, w_up.T, preferred_element_type=jnp.float32)
    heads = w_qkv.shape[1] // (3 * HD)
    mixed = record['mixed']
    mixed_flat = mixed.reshape(seqs * length, heads * HD)
    d_mixed = jnp.dot(d_branch, w_out.T, preferred_element_type=jnp.float32).astype(jnp.bfloat16)
    d_w_out = jnp.dot(mixed_flat.T, d_branch, preferred_element_type=jnp.float32)
    d_mixed = d_mixed.reshape(seqs, length, heads, HD)
    d_query, d_keys, d_values = lax.map(lambda xs: attend_backward(*xs), (record['query'], record['keys'], record['values'], mixed, d_mixed, record['lse'], segments))
    half = ROT // 2
    d_query = rotate(d_query, cos_t, sin_t, half, -1.0)
    d_keys = rotate(d_keys, cos_t, sin_t, half, -1.0)
    d_b_qv = jnp.stack([lax.optimization_barrier(jnp.sum(d_query, axis=(0, 1))), lax.optimization_barrier(jnp.sum(d_values, axis=(0, 1)))], axis=1).reshape(-1)
    d_proj = jnp.stack([d_query, d_keys, d_values], axis=3).reshape(seqs * length, heads * 3 * HD).astype(jnp.bfloat16)
    d_w_qkv = jnp.dot(attn_in.T, d_proj, preferred_element_type=jnp.float32)
    d_attn_in = jnp.dot(d_proj, w_qkv.T, preferred_element_type=jnp.float32)
    dx_attn, dg_attn, ds_attn = norm_backward(d_attn_in, record['attn_normal'], record['attn_scale'], gain[0])
    dx_mlp, dg_mlp, ds_mlp = norm_backward(d_mlp_in, record['mlp_normal'], record['mlp_scale'], gain[1])
    d_prev = d_hidden + dx_attn + dx_mlp
    big = (d_w_qkv, d_b_qv, d_w_out, d_w_up, d_b_up, d_w_down)
    small = (jnp.stack([dg_attn, dg_mlp]), jnp.stack([ds_attn, ds_mlp]), d_resid_bias)
    return (d_prev, big, small)

def reference(tokens_in, ln_gain, ln_bias, w_qkv, b_qv, w_out, b_resid, w_up, b_up, w_down, segments, cotangent):
    layers = w_qkv.shape[0]
    cos_t, sin_t = rotary_tables(positions(segments), ROT // 2)
    everything = (ln_gain, ln_bias, w_qkv, b_qv, w_out, b_resid, w_up, b_up, w_down)
    hidden = tokens_in.astype(jnp.float32)
    records = []
    for layer in range(layers):
        params = tuple((item[layer] for item in everything))
        hidden, record = layer_forward(hidden, params, cos_t, sin_t, segments)
        records.append(record)
    result = hidden.astype(jnp.bfloat16)
    grad = cotangent.astype(jnp.float32)
    bigs = [None] * layers
    smalls = [None] * layers
    for layer in reversed(range(layers)):
        params = tuple((item[layer] for item in everything))
        grad, bigs[layer], smalls[layer] = layer_backward(grad, params, records[layer], cos_t, sin_t, segments)
    big = tuple((jnp.stack([bigs[i][j] for i in range(layers)]) for j in range(6)))
    small = tuple((jnp.stack([smalls[i][j] for i in range(layers)]) for j in range(3)))
    return (result, grad, small[0], small[1], big[0], big[1], big[2], small[2], big[3], big[4], big[5])
```

```python
import functools

import jax
import jax.numpy as jnp
from jax import lax
from jax.experimental import pallas as pl
from jax.experimental.pallas import tpu as pltpu
from jax.sharding import PartitionSpec as P

HD = 64
ROT = 16
EPS = 1e-05
DOC = 512
LANES = 128
F32 = jnp.float32
BF16 = jnp.bfloat16


def order_of(n):
    return [d for d in range(n) if d % 2 == 0] + [d for d in range(n) if d % 2 == 1]


def swap(x, bit, n, axis="tensor"):
    return lax.ppermute(x, axis, [(i, i ^ bit) for i in range(n)])


def gather_rows(x, n):
    if n != 8:
        every = lax.all_gather(x, "tensor", axis=0)
        t = lax.axis_index("tensor")
        return jnp.take(every, jnp.asarray(order_of(n)) ^ t, axis=0).reshape(-1, x.shape[-1])
    half = x.shape[0] // 2
    a = swap(x, 2, n)
    b = swap(x, 4, n)
    d_lo = swap(b[:half], 2, n)
    d_hi = swap(a[half:], 4, n)
    near = jnp.concatenate([x, a, b], axis=0)
    far = jnp.concatenate([d_lo, d_hi], axis=0)
    return jnp.concatenate([near, far, swap(near, 1, n), swap(far, 1, n)], axis=0)


def scatter_rows(p, n):
    rows = p.shape[0] // n
    if n != 8:
        t = lax.axis_index("tensor")
        blocks = p.reshape(n, rows, -1)
        inverse = [order_of(n).index(d) for d in range(n)]
        blocks = jnp.take(blocks, jnp.asarray(inverse)[jnp.arange(n) ^ t], axis=0)
        return lax.psum_scatter(blocks.reshape(p.shape), "tensor", scatter_dimension=0, tiled=True).astype(F32)
    half = rows // 2
    other = swap(p[4 * rows :], 1, n)
    diag = (p[3 * rows : 4 * rows].astype(F32) + other[3 * rows :].astype(F32)).astype(BF16)
    e_x = swap(diag[:half], 4, n)
    e_y = swap(diag[half:], 2, n)
    h0 = p[:rows].astype(F32) + other[:rows].astype(F32)
    h2 = p[rows : 2 * rows].astype(F32) + other[rows : 2 * rows].astype(F32)
    h4 = p[2 * rows : 3 * rows].astype(F32) + other[2 * rows : 3 * rows].astype(F32)
    zero = jnp.zeros((half, p.shape[1]), F32)
    h2 = (h2 + jnp.concatenate([e_x.astype(F32), zero], axis=0)).astype(BF16)
    h4 = (h4 + jnp.concatenate([zero, e_y.astype(F32)], axis=0)).astype(BF16)
    return h0 + swap(h2, 2, n).astype(F32) + swap(h4, 4, n).astype(F32)


def sum_line(v, n):
    if n != 4:
        return lax.psum(v, "dp")
    z = lax.axis_index("dp")
    r = lax.ppermute(v, "dp", [(0, 1), (3, 2)])
    s = (v.astype(F32) + r.astype(F32)).astype(BF16)
    r = lax.ppermute(s, "dp", [(1, 2), (2, 1)])
    total = (s.astype(F32) + r.astype(F32)).astype(BF16)
    r = lax.ppermute(total, "dp", [(1, 0), (2, 3)])
    return jnp.where((z == 1) | (z == 2), total, r)


def sum_small(v, n, axis):
    if n & (n - 1):
        return lax.psum(v, axis)
    bit = 1
    while bit < n:
        v = v + swap(v, bit, n, axis)
        bit *= 2
    return v


def first_of_segment(segments):
    length = segments.shape[-1]
    index = jnp.broadcast_to(jnp.arange(length, dtype=jnp.int32), segments.shape)
    starts = jnp.concatenate(
        [jnp.ones_like(segments[:, :1]), (segments[:, 1:] != segments[:, :-1]).astype(jnp.int32)],
        axis=1,
    )
    first = lax.cummax(jnp.where(starts > 0, index, 0), axis=1)
    return index, first


def rotary_lanes(pos, width):
    half = ROT // 2
    lane = jnp.arange(width, dtype=jnp.int32) % HD
    freq = 10000.0 ** (-jnp.arange(half, dtype=F32) / half)
    freq = jnp.where(lane < ROT, freq[lane % half], 0.0)
    angle = pos.astype(F32)[:, None] * freq[None, :]
    return jnp.cos(angle), jnp.sin(angle)


def roll_lanes(x, shift):
    return pltpu.roll(x, shift % x.shape[1], 1)


def rotated(x, cos_t, sin_t, sign):
    half = ROT // 2
    lane = lax.broadcasted_iota(jnp.int32, x.shape, 1) % HD
    up = roll_lanes(x, -half)
    down = roll_lanes(x, half)
    turned = jnp.where(lane < half, -sign * up, sign * down)
    return x * cos_t + jnp.where(lane < ROT, turned, 0.0) * sin_t


def key_range(b, block):
    return max(0, (b * block - DOC) // block * block), (b + 1) * block


def block_mask(start, b, block, k0, k1):
    shape = (block, k1 - k0)
    rows = lax.broadcasted_iota(jnp.int32, shape, 0) + b * block
    cols = lax.broadcasted_iota(jnp.int32, shape, 1) + k0
    return (cols <= rows) & (cols >= start)


NT = (((1,), (1,)), ((), ()))
NN = (((1,), (0,)), ((), ()))
TN = (((0,), (0,)), ((), ()))


def mxu(a, b, dims):
    return lax.dot_general(a, b, dims, preferred_element_type=F32)


def forward_body(heads, rows, n, block, nat, inv, f_ref, gain_ref, shift_ref, w_ref, b_ref, cos_ref, sin_ref, start_ref,
                 qkv_ref, mixed_ref, lse_ref, proj_ref, mix_ref):
    length = f_ref.shape[0]
    width = w_ref.shape[1] // 3
    half = length // 2
    for i in range(2):
        at = pl.ds(i * half, half)
        a = (f_ref[at, :].astype(F32) * gain_ref[...] + shift_ref[...]).astype(BF16)
        proj_ref[at, :] = mxu(a, w_ref[...], NN) + b_ref[...]
    for i in range(n):
        src = pl.ds(i * rows, rows)
        dst = pl.ds(pl.multiple_of(nat[i] * rows, rows), rows)
        cos_t = cos_ref[dst, :]
        sin_t = sin_ref[dst, :]
        q = rotated(proj_ref[src, :width], cos_t, sin_t, 1.0)
        qkv_ref[dst, :width] = q.astype(BF16) * jnp.asarray(HD**-0.5, BF16)
        k = rotated(proj_ref[src, width : 2 * width], cos_t, sin_t, 1.0)
        qkv_ref[dst, width : 2 * width] = k.astype(BF16)
        qkv_ref[dst, 2 * width :] = proj_ref[src, 2 * width :].astype(BF16)
    lse_ref[...] = jnp.zeros_like(lse_ref)
    if heads * HD != width:
        mix_ref[...] = jnp.zeros_like(mix_ref)
    for b in range(length // block):
        k0, k1 = key_range(b, block)
        at = pl.ds(b * block, block)
        mask = block_mask(start_ref[at, :], b, block, k0, k1)
        for h in range(heads):
            lo = h * HD
            q = qkv_ref[at, lo : lo + HD]
            k = qkv_ref[k0:k1, width + lo : width + lo + HD]
            v = qkv_ref[k0:k1, 2 * width + lo : 2 * width + lo + HD]
            s = jnp.where(mask, mxu(q, k, NT), -1e30)
            top = jnp.max(s, axis=1, keepdims=True)
            e = jnp.exp(s - top)
            total = jnp.sum(e, axis=1, keepdims=True)
            mix_ref[at, lo : lo + HD] = mxu(e.astype(BF16), v, NN) / total
            lse_ref[at, h : h + 1] = top + jnp.log(total)
    for i in range(n):
        src = pl.ds(pl.multiple_of(nat[i] * rows, rows), rows)
        mixed_ref[pl.ds(i * rows, rows), :] = mix_ref[src, :].astype(BF16)


def backward_body(heads, rows, n, block, nat, inv, qkv_ref, mixed_ref, dmix_ref, lse_ref, cos_ref, sin_ref, start_ref,
                  dproj_ref, sums_ref, do_ref, delta_ref, dq_ref, dk_ref, dv_ref):
    length = qkv_ref.shape[0]
    width = qkv_ref.shape[1] // 3
    for i in range(n):
        src = pl.ds(i * rows, rows)
        dst = pl.ds(pl.multiple_of(nat[i] * rows, rows), rows)
        do = dmix_ref[src, :]
        do_ref[dst, :] = do
        both = mixed_ref[src, :].astype(F32) * do.astype(F32)
        for h in range(heads):
            delta_ref[dst, h : h + 1] = jnp.sum(both[:, h * HD : (h + 1) * HD], axis=1, keepdims=True)
    dk_ref[...] = jnp.zeros_like(dk_ref)
    dv_ref[...] = jnp.zeros_like(dv_ref)
    if heads * HD != width:
        dq_ref[...] = jnp.zeros_like(dq_ref)
    for b in range(length // block):
        k0, k1 = key_range(b, block)
        at = pl.ds(b * block, block)
        mask = block_mask(start_ref[at, :], b, block, k0, k1)
        for h in range(heads):
            lo = h * HD
            q = qkv_ref[at, lo : lo + HD]
            k = qkv_ref[k0:k1, width + lo : width + lo + HD]
            v = qkv_ref[k0:k1, 2 * width + lo : 2 * width + lo + HD]
            do = do_ref[at, lo : lo + HD]
            p = jnp.exp(jnp.where(mask, mxu(q, k, NT) - lse_ref[at, h : h + 1], -1e30))
            dp = mxu(do, v, NT)
            ds = (p * (dp - delta_ref[at, h : h + 1])).astype(BF16)
            dv_ref[k0:k1, lo : lo + HD] += mxu(p.astype(BF16), do, TN)
            dq_ref[at, lo : lo + HD] = mxu(ds, k, NN) * (HD**-0.5)
            dk_ref[k0:k1, lo : lo + HD] += mxu(ds, q, TN)
    totals = [jnp.zeros((1, width), F32)] * 3
    for i in range(n):
        dst = pl.ds(i * rows, rows)
        src = pl.ds(pl.multiple_of(nat[i] * rows, rows), rows)
        cos_t = cos_ref[src, :]
        sin_t = sin_ref[src, :]
        parts = [
            rotated(dq_ref[src, :], cos_t, sin_t, -1.0),
            rotated(dk_ref[src, :], cos_t, sin_t, -1.0),
            dv_ref[src, :],
        ]
        for j in range(3):
            totals[j] = totals[j] + jnp.sum(parts[j], axis=0, keepdims=True)
            for h in range(heads):
                lo = (3 * h + j) * HD
                dproj_ref[dst, lo : lo + HD] = parts[j][:, h * HD : (h + 1) * HD].astype(BF16)
    for j in range(3):
        sums_ref[j : j + 1, :] = totals[j]


def whole_arrays(body, outs, scratch, ins, flops):
    vmem = pl.BlockSpec(memory_space=pltpu.VMEM)
    smem = pl.BlockSpec(memory_space=pltpu.SMEM)
    nbytes = sum(a.size * a.dtype.itemsize for a in ins) + sum(o.size * o.dtype.itemsize for o in outs)
    return pl.pallas_call(
        body,
        out_shape=outs,
        in_specs=[smem, smem] + [vmem] * (len(ins) - 2),
        out_specs=[vmem] * len(outs),
        scratch_shapes=scratch,
        compiler_params=pltpu.CompilerParams(vmem_limit_bytes=48 * 1024 * 1024),
        cost_estimate=pl.CostEstimate(flops=flops, bytes_accessed=nbytes, transcendentals=0),
    )(*ins)


def attention_forward(plan, full, gain, shift, w, b):
    heads, rows, n = plan["heads"], plan["rows"], plan["n"]
    length = full.shape[0]
    width = w.shape[1] // 3
    block = min(256, length)
    outs = [
        jax.ShapeDtypeStruct((length, 3 * width), BF16),
        jax.ShapeDtypeStruct((length, width), BF16),
        jax.ShapeDtypeStruct((length, LANES), F32),
    ]
    scratch = [pltpu.VMEM((length, 3 * width), F32), pltpu.VMEM((length, width), F32)]
    ins = [plan["nat"], plan["inv"], full, gain[None], shift[None], w, b[None], plan["cos"], plan["sin"], plan["start"]]
    body = functools.partial(forward_body, heads, rows, n, block)
    return whole_arrays(body, outs, scratch, ins, 2 * length * full.shape[1] * 3 * width)


def attention_backward(plan, qkv, mixed, dmix, lse):
    heads, rows, n = plan["heads"], plan["rows"], plan["n"]
    length = qkv.shape[0]
    width = qkv.shape[1] // 3
    block = min(256, length)
    outs = [jax.ShapeDtypeStruct((length, 3 * heads * HD), BF16), jax.ShapeDtypeStruct((3, width), F32)]
    scratch = [
        pltpu.VMEM((length, width), BF16),
        pltpu.VMEM((length, LANES), F32),
        pltpu.VMEM((length, width), F32),
        pltpu.VMEM((length, width), F32),
        pltpu.VMEM((length, width), F32),
    ]
    ins = [plan["nat"], plan["inv"], qkv, mixed, dmix, lse, plan["cos"], plan["sin"], plan["start"]]
    body = functools.partial(backward_body, heads, rows, n, block)
    return whole_arrays(body, outs, scratch, ins, 10 * length * 3 * block * heads * HD)


def normalized(rows):
    mean = jnp.mean(rows, axis=-1, keepdims=True)
    centred = rows - mean
    scale = lax.rsqrt(jnp.mean(centred * centred, axis=-1, keepdims=True) + EPS)
    return centred * scale, scale


def gelu_parts(pre):
    cdf = 0.5 * (1.0 + lax.erf(pre * 0.7071067811865476))
    density = jnp.exp(-0.5 * pre * pre) * 0.3989422804014327
    return pre * cdf, cdf + pre * density


def dot(a, b):
    return jnp.dot(a, b, preferred_element_type=F32)


def dot_nt(a, b):
    return lax.dot_general(a, b, NT, preferred_element_type=F32)


def dot_tn(a, b):
    return lax.dot_general(a, b, TN, preferred_element_type=F32)


def heads_apart(w, heads, width):
    parts = w.reshape(w.shape[0], heads, 3, HD).transpose(0, 2, 1, 3).reshape(w.shape[0], 3, heads * HD)
    parts = jnp.pad(parts, ((0, 0), (0, 0), (0, width - heads * HD)))
    return parts.reshape(w.shape[0], 3 * width)


def local(n, dp, tokens_in, ln_gain, ln_bias, w_qkv, b_qv, w_out, b_resid, w_up, b_up, w_down, segments, cotangent):
    layers = w_qkv.shape[0]
    rows = tokens_in.shape[0]
    heads = w_qkv.shape[2] // (3 * HD)
    width = -(-heads * HD // LANES) * LANES
    index, first = first_of_segment(segments)
    cos_t, sin_t = rotary_lanes((index - first)[0], width)
    t = lax.axis_index("tensor")
    order = order_of(n)
    plan = {
        "heads": heads,
        "rows": rows,
        "n": n,
        "nat": (jnp.asarray(order, jnp.int32) ^ t).astype(jnp.int32),
        "inv": (jnp.asarray(order, jnp.int32) ^ t).astype(jnp.int32),
        "cos": cos_t,
        "sin": sin_t,
        "start": first[0][:, None],
    }
    w_apart, b_apart = [], []
    for l in range(layers):
        w_apart.append(heads_apart(w_qkv[l], heads, width))
        bias = b_qv[l].reshape(heads, 2, HD)
        bias = jnp.stack([bias[:, 0], jnp.zeros_like(bias[:, 0]), bias[:, 1]], axis=1)
        b_apart.append(heads_apart(bias.reshape(1, heads * 3 * HD), heads, width)[0])

    def down_weights(w):
        pad = width - heads * HD
        return jnp.pad(w, ((0, pad), (0, 0))) if pad else w

    hidden = tokens_in.astype(F32)
    records = []
    for l in range(layers):
        normal, scale = normalized(hidden)
        full = gather_rows(normal.astype(BF16), n)
        mlp_in = (full.astype(F32) * ln_gain[l, 1] + ln_bias[l, 1]).astype(BF16)
        act, slope = gelu_parts(dot(mlp_in, w_up[l]) + b_up[l])
        act = act.astype(BF16)
        qkv, mixed, lse = attention_forward(plan, full, ln_gain[l, 0], ln_bias[l, 0], w_apart[l], b_apart[l])
        partial = dot(mixed, down_weights(w_out[l])) + dot(act, w_down[l])
        hidden = hidden + scatter_rows(partial.astype(BF16), n) + b_resid[l]
        records.append((normal, scale, full, act, slope, qkv, mixed, lse))
    result = hidden.astype(BF16)

    grad = cotangent.astype(F32)
    g_full = gather_rows(cotangent, n)
    pieces = [None] * layers
    norm_rows, bias_rows = [], []
    for l in reversed(range(layers)):
        normal, scale, full, act, slope, qkv, mixed, lse = records[l]
        if l + 1 < layers:
            g_full = gather_rows(grad.astype(BF16), n)
        g_down = sum_line(dot_tn(act, g_full).astype(BF16), dp)
        d_pre = dot_nt(g_full, w_down[l]) * slope
        d_pre_b = d_pre.astype(BF16)
        up_sum = jnp.sum(d_pre, axis=0)
        up_raw = dot_tn(full, d_pre_b)
        g_up = ln_gain[l, 1][:, None] * up_raw + ln_bias[l, 1][:, None] * up_sum[None, :]
        g_up = sum_line(g_up.astype(BF16), dp)
        d_mixed = dot_nt(g_full, down_weights(w_out[l])).astype(BF16)
        g_out = sum_line(dot_tn(mixed[:, : heads * HD], g_full).astype(BF16), dp)
        d_proj, sums = attention_backward(plan, qkv, mixed, d_mixed, lse)
        q_sum, k_sum, v_sum = [sums[j, : heads * HD].reshape(heads, HD) for j in range(3)]
        proj_sum = jnp.stack([q_sum, k_sum, v_sum], axis=1).reshape(-1)
        weighted = dot_nt(d_proj, w_qkv[l]) * ln_gain[l, 0] + dot_nt(d_pre_b, w_up[l]) * ln_gain[l, 1]
        own = scatter_rows(weighted.astype(BF16), n)
        qkv_raw = dot_tn(full, d_proj)
        g_qkv = ln_gain[l, 0][:, None] * qkv_raw + ln_bias[l, 0][:, None] * proj_sum[None, :]
        g_qkv = sum_line(g_qkv.astype(BF16), dp)
        norm_rows.append(
            jnp.stack(
                [
                    jnp.sum(w_qkv[l].astype(F32) * qkv_raw, axis=1),
                    jnp.sum(w_up[l].astype(F32) * up_raw, axis=1),
                    jnp.sum(w_qkv[l].astype(F32) * proj_sum, axis=1),
                    jnp.sum(w_up[l].astype(F32) * up_sum, axis=1),
                    jnp.sum(grad, axis=0),
                ]
            )
        )
        bias_rows.append(jnp.concatenate([jnp.stack([q_sum, v_sum], axis=1).reshape(-1), up_sum]))
        pieces[l] = (g_qkv, g_out, g_up, g_down)
        inner = own - jnp.mean(own, axis=-1, keepdims=True) - normal * jnp.mean(own * normal, axis=-1, keepdims=True)
        grad = grad + inner * scale

    small = sum_small(jnp.concatenate(norm_rows[::-1], axis=0), n, "tensor")
    tail = jnp.stack(bias_rows[::-1])
    flat = sum_small(jnp.concatenate([small.reshape(-1), tail.reshape(-1)]), dp, "dp")
    small = flat[: small.size].reshape(layers, 5, -1)
    tail = flat[small.size :].reshape(tail.shape)
    qv = heads * 2 * HD
    big = [jnp.stack([pieces[l][j].astype(F32) for l in range(layers)]) for j in range(4)]
    return (
        result,
        grad,
        small[:, 0:2],
        small[:, 2:4],
        big[0],
        tail[:, :qv],
        big[1],
        small[:, 4],
        big[2],
        tail[:, qv:],
        big[3],
    )


def solution(mesh):
    rows = P(("dp", "tensor"), None)
    columns = P(None, None, "tensor")
    middle = P(None, "tensor", None)
    lanes = P(None, "tensor")
    placed = (rows, P(), P(), columns, lanes, middle, P(), columns, lanes, middle, P("dp", None), rows)
    return jax.shard_map(
        functools.partial(local, mesh.shape["tensor"], mesh.shape["dp"]),
        mesh=mesh,
        in_specs=placed,
        out_specs=(rows, rows, P(), P(), columns, lanes, middle, P(), columns, lanes, middle),
        check_vma=False,
    )
```
